32 devices in a mesh: row: 4 (over y, x), col: 8 (over z, core).
Axes of the slice: x: 2, y: 2, z: 4, core: 2. Of those that a mesh axis runs over, the one named last changes fastest.
Arguments:
- messages: bfloat16 [4, 8, 1024, 512], P('row', 'col'), may hold values from -6 to 6
- targets: int32 [4, 8, 1024], P('row', 'col'), may hold values from 0 to 255
- reverse_rows: int32 [4, 8, 8, 128], P('row', 'col'), may hold values from 0 to 127, as said below
- nodes: bfloat16 [8, 256, 512], P('col', 'row'), may hold values from -6 to 6
- w_in: bfloat16 [2, 1536, 512], replicated, may hold values from -0.15625 to 0.15625
- w_res: bfloat16 [2, 2, 2, 512, 512], replicated, may hold values from -0.25 to 0.25
- w_node: bfloat16 [2, 512, 512], replicated, may hold values from -0.25 to 0.25
Outputs:
- edge_out: bfloat16 [4, 8, 1024, 512], P('row', 'col')
- node_out: bfloat16 [8, 256, 512], P('col', 'row')
The draws below stay inside these ranges and needn't reach their ends.
Inputs may be any that keep to these rules, and one draw needn't show every extreme that they name: reverse_rows[s, c, k] is a permutation of the block's rows, and the reversal is an involution: the reversed edge of the reversed edge is the edge itself.
All inputs are finite; a program needn't handle non-finite values.
Results may differ from the reference program's by a relative error of at most 0.0065.
Values may be sent and summed in bfloat16 or wider, within the bound.
No kernel may reach another device: no remote copies, remote signals or barrier semaphores. Data moves between devices by JAX's collectives and lax.ppermute only.
A program may use at most 64 MiB of HBM per device.

```python
import math
import jax
import jax.numpy as jnp
from jax import lax

D = 512
BLOCK = 128
NBLK = 8
ITERS = 2
NODES_DEV = 64
EDGES_DEV = 1024
SLABS = 4
GROUPS = 8
NODES = 256


def draw_reverse_rows(key, part):
    key_list = jax.random.split(jax.random.fold_in(key, 4711), SLABS * GROUPS * 4)
    perms = jax.vmap(lambda one_key: jax.random.permutation(one_key, BLOCK))(key_list)
    perms = perms.reshape(SLABS, GROUPS, 4, BLOCK).astype(jnp.int32)
    inverse = jnp.argsort(perms, axis=-1, stable=True).astype(jnp.int32)
    result = [perms[:, :, 0], inverse[:, :, 0]]
    for offset in range(1, 4):
        result.append(perms[:, :, offset])
        result.append(jnp.roll(inverse[:, :, offset], offset, axis=1))
    return jnp.stack(result, axis=2).astype(jnp.int32)


def plant(entries, own_key, least, high):
    longest = entries.shape.index(max(entries.shape))
    spots = []
    for shift in (0, 1):
        where = [jax.random.randint(jax.random.fold_in(own_key, axis), (), 0, length) for axis, length in enumerate(entries.shape)]
        where[longest] = (where[longest] + shift) % entries.shape[longest]
        spots.append(tuple(where))
    return entries.at[spots[0]].set(least).at[spots[1]].set(high)


def block_levels(key, shape, pieces, low, largest):
    factor_of = 1.0
    for dim, blocks in pieces:
        draws = jax.random.uniform(jax.random.fold_in(jax.random.fold_in(key, 6), dim), (blocks,), jnp.float32, low / len(pieces), largest / len(pieces))
        factor_of = factor_of * jnp.repeat(jnp.exp(draws), shape[dim] // blocks).reshape((-1,) + (1,) * (len(shape) - 1 - dim))
    return factor_of


def bell_draw(rng, extent, scale, most, shards=(), held_as=jnp.bfloat16):
    level = block_levels(rng, extent, shards, -0.22, 0.18) if shards else 1.0
    entries = jax.random.normal(rng, extent, jnp.float32) * scale * level
    return jnp.minimum(jnp.maximum(entries, -most), most).astype(held_as)


def setup_inputs(seed: int = 0) -> dict:
    seeds = jax.random.split(jax.random.key(seed), 8)
    messages = bell_draw(seeds[0], (SLABS, GROUPS, EDGES_DEV, D), 1.0, 6.0, ((0, 4), (1, 8)))
    targets = plant(jax.random.randint(seeds[1], (SLABS, GROUPS, EDGES_DEV), 0, NODES), jax.random.fold_in(seeds[1], 1), 0, NODES - 1).astype(jnp.int32)
    reverse_rows = draw_reverse_rows(jax.random.fold_in(seeds[7], 71), 0)
    nodes = bell_draw(seeds[3], (GROUPS, NODES, D), 1.0, 6.0, ((0, 8), (1, 4)))
    w_in = bell_draw(seeds[4], (ITERS, 3 * D, D), (3 * D) ** -0.5, 0.15625)
    w_res = bell_draw(seeds[5], (ITERS, 2, 2, D, D), D ** -0.5, 0.25)
    w_node = bell_draw(seeds[6], (ITERS, D, D), D ** -0.5, 0.25)
    return {"messages": messages, "targets": targets, "reverse_rows": reverse_rows, "nodes": nodes, "w_in": w_in, "w_res": w_res, "w_node": w_node}


OFFSETS = (0, 0, 1, -1, 2, -2, 3, -3)
ROOT_HALF = 0.7071067811865476

def reverse_all(stack, reverse_rows):
    blocks = stack.reshape(SLABS, GROUPS, NBLK, BLOCK, stack.shape[-1])
    result = []
    for index in range(NBLK):
        source = jnp.roll(blocks[:, :, index ^ 1], -OFFSETS[index], axis=1)
        row_order = reverse_rows[:, :, index, :].astype(jnp.int32)
        result.append(jnp.take_along_axis(source, row_order[:, :, :, None], axis=2))
    return jnp.stack(result, axis=2).reshape(stack.shape)

def edge_layer(m_rev, h_src, h_tgt, current, w_first, w_blocks):
    joined = jnp.concatenate([m_rev, h_src, h_tgt], axis=-1)
    hidden = jax.nn.silu(jnp.dot(joined, w_first, preferred_element_type=jnp.float32)).astype(jnp.bfloat16)
    summed = hidden.astype(jnp.float32)
    for index in range(2):
        inner_act = jax.nn.silu(jnp.dot(hidden, w_blocks[index, 0], preferred_element_type=jnp.float32)).astype(jnp.bfloat16)
        summed = (hidden.astype(jnp.float32) + jax.nn.silu(jnp.dot(inner_act, w_blocks[index, 1], preferred_element_type=jnp.float32))) * ROOT_HALF
        if index == 0:
            hidden = summed.astype(jnp.bfloat16)
    return ((current.astype(jnp.float32) + summed) * ROOT_HALF).astype(jnp.bfloat16)

def reference(messages, targets, reverse_rows, nodes, w_in, w_res, w_node):
    agg_scale = 1.0 / math.sqrt(EDGES_DEV // NODES_DEV)
    current = messages
    node_flat = nodes.reshape(GROUPS * NODES, D)
    group_ids = (targets + (jnp.arange(GROUPS, dtype=jnp.int32) * NODES)[None, :, None]).astype(jnp.int32)

    def add_slab(running, pair):
        slab_rows, slab_ids = pair
        return (running + jax.ops.segment_sum(slab_rows.reshape(-1, D).astype(jnp.float32), slab_ids.reshape(-1), num_segments=GROUPS * NODES), None)
    for layer in range(ITERS):
        gathered_sum, _ = lax.scan(add_slab, jnp.zeros((GROUPS * NODES, D), jnp.float32), (current, group_ids))
        scaled = (gathered_sum * agg_scale).astype(jnp.bfloat16)
        update = jax.nn.silu(jnp.dot(scaled, w_node[layer], preferred_element_type=jnp.float32))
        node_flat = (node_flat.astype(jnp.float32) + update).astype(jnp.bfloat16)
        h_tgt = jnp.take(node_flat, group_ids, axis=0)
        m_rev = reverse_all(current, reverse_rows)
        h_src = reverse_all(h_tgt, reverse_rows)
        w_first = w_in[layer]
        w_blocks = w_res[layer]

        def slab_layer(items):
            return edge_layer(items[0], items[1], items[2], items[3], w_first, w_blocks)
        current = lax.map(slab_layer, (m_rev, h_src, h_tgt, current))
    return (current, node_flat.reshape(GROUPS, NODES, D))
```

```python
import functools
import math

import jax
import jax.numpy as jnp
from jax import lax
from jax.experimental import pallas as pl
from jax.experimental.pallas import tpu as pltpu
from jax.sharding import PartitionSpec as P

OFFSETS = (0, 0, 1, -1, 2, -2, 3, -3)
ROOT_HALF = 0.7071067811865476
PAIRS = len(OFFSETS) // 2
F32 = jnp.float32
BF16 = jnp.bfloat16


def dot(a, b):
    return jnp.dot(a, b, preferred_element_type=F32)


def silu(v):
    half = 0.5 * v
    return half + half * jnp.tanh(half)


def call(body, outs, args, flops, smem=()):
    specs = [
        pl.BlockSpec(memory_space=pltpu.SMEM if i in smem else pltpu.VMEM)
        for i in range(len(args))
    ]
    moved = sum(math.prod(a.shape) * a.dtype.itemsize for a in list(args) + list(outs))
    return pl.pallas_call(
        body,
        out_shape=tuple(jax.ShapeDtypeStruct(o.shape, o.dtype) for o in outs),
        in_specs=specs,
        out_specs=tuple(pl.BlockSpec(memory_space=pltpu.VMEM) for _ in outs),
        compiler_params=pltpu.CompilerParams(vmem_limit_bytes=40 << 20),
        cost_estimate=pl.CostEstimate(flops=flops, bytes_accessed=moved, transcendentals=0),
    )(*args)


def partial_body(targets_ref, m_ref, *outs):
    share = outs[0].shape[0]
    edges = m_ref.shape[0]
    for k, out in enumerate(outs):
        points = lax.broadcasted_iota(jnp.int32, (share, edges), 0) + k * share
        hot = (points == targets_ref[...]).astype(F32).astype(BF16)
        out[...] = dot(hot, m_ref[...]).astype(out.dtype)


def update_body(scale, *refs):
    sums, (node_ref, w_ref, out) = refs[:-3], refs[-3:]
    total = sums[0][...].astype(F32)
    for ref in sums[1:]:
        total = total + ref[...].astype(F32)
    z = (total * scale).astype(BF16)
    out[...] = (node_ref[...].astype(F32) + silu(dot(z, w_ref[...]))).astype(BF16)


def send_body(count, hot_ref, m_ref, rows_ref, w_ref, *refs):
    shares, outs = refs[:count], refs[count:]
    table = jnp.concatenate([ref[...] for ref in shares], axis=0)
    width = m_ref.shape[1]
    block = outs[0].shape[0]
    place = lax.broadcasted_iota(jnp.int32, (block, block), 0)
    for pair in reversed(range(PAIRS)):
        rows = pl.ds(pair * 2 * block, 2 * block)
        h_tgt = dot(hot_ref[rows, :], table).astype(BF16)
        mixed = dot(m_ref[rows, :], w_ref[:width, :]) + dot(h_tgt, w_ref[width : 2 * width, :])
        mixed = mixed.astype(BF16)
        for half in range(2):
            k = pair * 2 + half
            order = (place == rows_ref[k : k + 1, :]).astype(F32).astype(BF16)
            outs[k][...] = dot(order, mixed[half * block : (half + 1) * block]).astype(BF16)


def edge_rows(first, m_rows, w_ref):
    x1 = silu(first).astype(BF16)
    a1 = silu(dot(x1, w_ref[0, 0])).astype(BF16)
    x2 = ((x1.astype(F32) + silu(dot(a1, w_ref[0, 1]))) * ROOT_HALF).astype(BF16)
    a2 = silu(dot(x2, w_ref[1, 0])).astype(BF16)
    x3 = (x2.astype(F32) + silu(dot(a2, w_ref[1, 1]))) * ROOT_HALF
    return ((m_rows.astype(F32) + x3) * ROOT_HALF).astype(BF16)


def edge_body(count, pair, low_ref, high_ref, hot_ref, m_ref, w_in_ref, w_ref, *refs):
    shares, out = refs[:count], refs[-1]
    block, width = low_ref.shape
    table = jnp.concatenate([ref[...] for ref in shares], axis=0)
    rows = pl.ds(pair * 2 * block, 2 * block)
    h_tgt = dot(hot_ref[rows, :], table).astype(BF16)
    got = jnp.concatenate([low_ref[...], high_ref[...]], axis=0).astype(F32)
    first = got + dot(h_tgt, w_in_ref[2 * width :, :])
    out[...] = edge_rows(first, m_ref[rows, :], w_ref)


def partner_perm(count, k):
    if count & (count - 1) == 0:
        return [(s, s ^ k) for s in range(count)]
    return [(s, (s + k) % count) for s in range(count)]


def col_shift(value, steps):
    count = lax.axis_size("col")
    return lax.ppermute(value, "col", [(s, (s + steps) % count) for s in range(count)])


def shards(messages, targets, reverse_rows, nodes, w_in, w_res, w_node):
    m = messages[0, 0]
    rows_order = reverse_rows[0, 0]
    share_h = nodes[0]
    edges, width = m.shape
    share = share_h.shape[0]
    block = rows_order.shape[1]
    count = lax.axis_size("row")
    scale = 1.0 / math.sqrt(edges // share)
    me = lax.axis_index("row")
    tgt = targets[0, 0]
    if count & (count - 1) == 0:
        own = ((tgt // share) ^ me) * share + tgt % share
    else:
        own = ((tgt // share - me) % count) * share + tgt % share
    hot = (own[:, None] == jnp.arange(count * share, dtype=jnp.int32)[None, :]).astype(BF16)
    own = own[None, :]
    points = count * share
    sds = jax.ShapeDtypeStruct
    for layer in range(w_in.shape[0]):
        sums = call(
            partial_body,
            [sds((share, width), F32 if k == 0 else BF16) for k in range(count)],
            (own, m),
            2 * points * edges * width,
        )
        got = [sums[0]]
        for k in range(1, count):
            got.append(lax.ppermute(sums[k], "row", partner_perm(count, k)))
        (share_h,) = call(
            functools.partial(update_body, scale),
            [sds((share, width), BF16)],
            (*got, share_h, w_node[layer]),
            2 * share * width * width,
        )
        table = [share_h]
        for k in range(1, count):
            back = [(b, a) for a, b in partner_perm(count, k)]
            table.append(lax.ppermute(share_h, "row", back))
        sent = call(
            functools.partial(send_body, count),
            [sds((block, width), BF16)] * len(OFFSETS),
            (hot, m, rows_order, w_in[layer], *table),
            2 * edges * width * (2 * width + points),
        )
        received = [None] * len(OFFSETS)
        for k in reversed(range(len(OFFSETS))):
            received[k ^ 1] = col_shift(sent[k], OFFSETS[k]) if OFFSETS[k] else sent[k]
        parts = []
        for pair in range(PAIRS):
            (part,) = call(
                functools.partial(edge_body, count, pair),
                [sds((2 * block, width), BF16)],
                (received[2 * pair], received[2 * pair + 1], hot, m, w_in[layer], w_res[layer], *table),
                2 * 2 * block * width * (5 * width + points),
            )
            parts.append(part)
        m = jnp.concatenate(parts, axis=0)
    return (m[None, None], share_h[None])


def solution(mesh):
    in_specs = (
        P("row", "col", None, None),
        P("row", "col", None),
        P("row", "col", None, None),
        P("col", "row", None),
        P(),
        P(),
        P(),
    )
    out_specs = (P("row", "col", None, None), P("col", "row", None))
    return jax.shard_map(shards, mesh=mesh, in_specs=in_specs, out_specs=out_specs, check_vma=False)
```

```python
import functools
import math

import jax
import jax.numpy as jnp
from jax import lax
from jax.experimental import pallas as pl
from jax.experimental.pallas import tpu as pltpu
from jax.sharding import PartitionSpec as P

OFFSETS = (0, 0, 1, -1, 2, -2, 3, -3)
ROOT_HALF = 0.7071067811865476
PAIRS = len(OFFSETS) // 2
F32 = jnp.float32
BF16 = jnp.bfloat16


def dot(a, b):
    return jnp.dot(a, b, preferred_element_type=F32)


def silu(v):
    half = 0.5 * v
    return half + half * jnp.tanh(half)


def call(body, outs, args, flops, place=None, aliased=False):
    specs = [pl.BlockSpec(memory_space=pltpu.VMEM) for _ in args]
    out_specs = tuple(pl.BlockSpec(memory_space=pltpu.VMEM) for _ in outs)
    grid, aliases = {}, {}
    if place is not None:
        rows, at = place
        out_specs = (pl.BlockSpec((rows, outs[0].shape[1]), lambda i: (at, 0)),)
        grid = {"grid": (1,)}
        if aliased:
            specs[-1] = pl.BlockSpec(memory_space=pl.ANY)
            aliases = {len(args) - 1: 0}
    moved = sum(math.prod(a.shape) * a.dtype.itemsize for a in list(args) + list(outs))
    return pl.pallas_call(
        body,
        out_shape=tuple(jax.ShapeDtypeStruct(o.shape, o.dtype) for o in outs),
        in_specs=specs,
        out_specs=out_specs,
        input_output_aliases=aliases,
        compiler_params=pltpu.CompilerParams(vmem_limit_bytes=32 << 20),
        cost_estimate=pl.CostEstimate(flops=flops, bytes_accessed=moved, transcendentals=0),
        **grid,
    )(*args)


def hot_rows(targets, first, count):
    points = lax.broadcasted_iota(jnp.int32, (count, targets.shape[1]), 0) + first
    return (points == targets).astype(F32).astype(BF16)


def partial_body(targets_ref, m_ref, *outs):
    share = outs[0].shape[0]
    for k, out in enumerate(outs):
        hot = hot_rows(targets_ref[...], k * share, share)
        out[...] = dot(hot, m_ref[...]).astype(out.dtype)


def update_body(scale, *refs):
    sums, (node_ref, w_ref, out) = refs[:-3], refs[-3:]
    total = sums[0][...].astype(F32)
    for ref in sums[1:]:
        total = total + ref[...].astype(F32)
    z = (total * scale).astype(BF16)
    out[...] = (node_ref[...].astype(F32) + silu(dot(z, w_ref[...]))).astype(BF16)


def swapped(ref, bit, share):
    count = ref.shape[0] // share
    parts = [ref[(k ^ bit) * share : (k ^ bit) * share + share, :] for k in range(count)]
    return jnp.concatenate(parts, axis=0).astype(F32)


def add_body(bits, share, *refs):
    count = len(bits)
    for p, bit in enumerate(bits):
        total = refs[p][...] + swapped(refs[count + p], bit, share)
        refs[2 * count + 2 * p][...] = total
        refs[2 * count + 2 * p + 1][...] = total.astype(BF16)


def update_all_body(bits, share, scale, *refs):
    count = len(bits)
    (w_ref, out), nodes = refs[-2:], refs[2 * count : -2]
    totals = [refs[p][...] + swapped(refs[count + p], bit, share) for p, bit in enumerate(bits)]
    z = (jnp.concatenate(totals, axis=1) * scale).astype(BF16)
    old = jnp.concatenate([ref[...] for ref in nodes], axis=0).astype(F32)
    out[...] = (old + silu(dot(z, w_ref[...]))).astype(BF16)


def pre_body(*refs):
    (w_ref, out), at = refs[-2:], 0
    for ref in refs[:-2]:
        rows, width = ref.shape
        out[at : at + rows, :] = dot(ref[...], w_ref[:width, :])
        at += rows


def joined(refs):
    if len(refs) == 1:
        return refs[0][...]
    return jnp.concatenate([ref[...] for ref in refs], axis=0)


def send_body(pairs, hot_ref, pre_ref, order_ref, w_ref, *refs):
    shares, outs = refs[: -2 * len(pairs)], refs[-2 * len(pairs) :]
    table = joined(shares)
    block, width = outs[0].shape
    place = lax.broadcasted_iota(jnp.int32, (block, block), 0)
    for i, pair in enumerate(pairs):
        rows = pl.ds(pair * 2 * block, 2 * block)
        h_tgt = dot(hot_ref[rows, :], table).astype(BF16)
        mixed = pre_ref[rows, :] + dot(h_tgt, w_ref[width : 2 * width, :])
        mixed = mixed.astype(BF16)
        for half in range(2):
            k = pair * 2 + half
            order = (place == order_ref[k : k + 1, :]).astype(F32).astype(BF16)
            outs[2 * i + half][...] = dot(order, mixed[half * block : (half + 1) * block]).astype(BF16)


def target_body(hot_ref, w_ref, *refs):
    shares, out = refs[:-1], refs[-1]
    width = out.shape[1]
    h_tgt = dot(hot_ref[...], joined(shares)).astype(BF16)
    out[...] = dot(h_tgt, w_ref[2 * width :, :])


def edge_rows(pair, m_at, low_ref, high_ref, part_ref, m_ref, w_ref):
    block = low_ref.shape[0]
    rows = pl.ds(pair * 2 * block, 2 * block)
    got = jnp.concatenate([low_ref[...], high_ref[...]], axis=0).astype(F32)
    x1 = silu(got + part_ref[rows, :]).astype(BF16)
    a1 = silu(dot(x1, w_ref[0, 0])).astype(BF16)
    x2 = ((x1.astype(F32) + silu(dot(a1, w_ref[0, 1]))) * ROOT_HALF).astype(BF16)
    a2 = silu(dot(x2, w_ref[1, 0])).astype(BF16)
    x3 = (x2.astype(F32) + silu(dot(a2, w_ref[1, 1]))) * ROOT_HALF
    old = m_ref[pl.ds(m_at, 2 * block), :].astype(F32)
    return ((old + x3) * ROOT_HALF).astype(BF16)


def edge_body(pair, m_at, low_ref, high_ref, part_ref, m_ref, w_ref, *refs):
    refs[-1][...] = edge_rows(pair, m_at, low_ref, high_ref, part_ref, m_ref, w_ref)


def edge_sum_body(pair, m_at, first, low_ref, high_ref, part_ref, m_ref, w_ref, targets_ref, *refs):
    outs = refs if first else refs[1:]
    new = edge_rows(pair, m_at, low_ref, high_ref, part_ref, m_ref, w_ref)
    outs[0][...] = new
    block = low_ref.shape[0]
    targets = targets_ref[:, pair * 2 * block : (pair + 1) * 2 * block]
    total = dot(hot_rows(targets, 0, outs[1].shape[0]), new)
    if not first:
        total = total + refs[0][...]
    if len(outs) == 2:
        outs[1][...] = total
        return
    at = 0
    for exact, sent in zip(outs[1::2], outs[2::2]):
        piece = total[:, at : at + exact.shape[1]]
        exact[...] = piece
        sent[...] = piece.astype(BF16)
        at += exact.shape[1]


def partner_perm(count, k):
    if count & (count - 1) == 0:
        return [(s, s ^ k) for s in range(count)]
    return [(s, (s + k) % count) for s in range(count)]


def row_move(value, k):
    return lax.ppermute(value, "row", partner_perm(lax.axis_size("row"), k))


def row_move_back(value, k):
    pairs = partner_perm(lax.axis_size("row"), k)
    return lax.ppermute(value, "row", [(b, a) for a, b in pairs])


def col_shift(value, steps):
    count = lax.axis_size("col")
    return lax.ppermute(value, "col", [(s, (s + steps) % count) for s in range(count)])


def column_pieces(width, count):
    lanes = width // 128
    sizes = [lanes // count + (p < lanes % count) for p in range(count)]
    return [128 * size for size in sizes]


def sds(rows, width, dtype):
    return jax.ShapeDtypeStruct((rows, width), dtype)


def shards(messages, targets, reverse_rows, nodes, w_in, w_res, w_node):
    m = messages[0, 0]
    order = reverse_rows[0, 0]
    share_h = nodes[0]
    edges, width = m.shape
    share = share_h.shape[0]
    block = order.shape[1]
    pair_rows = 2 * block
    count = lax.axis_size("row")
    points = count * share
    scale = 1.0 / math.sqrt(edges // share)
    me = lax.axis_index("row")
    tgt = targets[0, 0]
    power = count & (count - 1) == 0 and count > 1
    if power:
        own = ((tgt // share) ^ me) * share + tgt % share
    else:
        own = ((tgt // share - me) % count) * share + tgt % share
    hot = (own[:, None] == jnp.arange(points, dtype=jnp.int32)[None, :]).astype(BF16)
    own = own[None, :]
    rounds = count.bit_length() - 1
    pieces = column_pieces(width, rounds) if power else []
    layers = w_in.shape[0]
    product = 2 * pair_rows * width * width
    m_parts = [(m, pair * pair_rows) for pair in range(PAIRS)]
    table, sums = None, None
    for layer in range(layers):
        whole = [m] if m is not None else [part for part, _ in m_parts]
        if sums is None:
            if m is None:
                m = jnp.concatenate(whole, axis=0)
            got = list(
                call(
                    partial_body,
                    [sds(share, width, F32 if k == 0 else BF16) for k in range(count)],
                    (own, m),
                    2 * points * edges * width,
                )
            )
            got = got[:1] + [row_move(got[k], k) for k in range(1, count)]
            (share_h,) = call(
                functools.partial(update_body, scale),
                [sds(share, width, BF16)],
                (*got, share_h, w_node[layer]),
                2 * share * width * width,
            )
            table = [share_h] + [row_move_back(share_h, k) for k in range(1, count)]
        else:
            for r in range(rounds):
                bits = [1 << ((p + r) % rounds) for p in range(rounds)]
                got = [row_move(sums[2 * p + 1], bit) for p, bit in enumerate(bits)]
                if r < rounds - 1:
                    sums = call(
                        functools.partial(add_body, bits, share),
                        [sds(points, piece, t) for piece in pieces for t in (F32, BF16)],
                        (*sums[::2], *got),
                        points * width,
                    )
            table = call(
                functools.partial(update_all_body, bits, share, scale),
                [sds(points, width, BF16)],
                (*sums[::2], *got, *table, w_node[layer]),
                2 * points * width * width,
            )
            share_h = table[0][:share]
        (pre,) = call(
            pre_body, [sds(edges, width, F32)], (*whole, w_in[layer]), PAIRS * product
        )
        sent = [None] * len(OFFSETS)
        for pairs in ([3], [2], [1], [0]):
            blocks = [2 * pair + half for pair in pairs for half in range(2)]
            outs = call(
                functools.partial(send_body, pairs),
                [sds(block, width, BF16)] * len(blocks),
                (hot, pre, order, w_in[layer], *table),
                len(pairs) * 2 * product,
            )
            for k, out in zip(blocks, outs):
                sent[k ^ 1] = col_shift(out, OFFSETS[k]) if OFFSETS[k] else out
        (part,) = call(
            target_body, [sds(edges, width, F32)], (hot, w_in[layer], *table), PAIRS * product * 2
        )
        m_next, sums = [None] * PAIRS, None
        last = layer == layers - 1
        final = None
        for pair in (0, 3, 2, 1):
            source, at = m_parts[pair]
            args = (sent[2 * pair], sent[2 * pair + 1], part, source, w_res[layer])
            if last:
                final = call(
                    functools.partial(edge_body, pair, at),
                    [sds(edges, width, BF16)],
                    args + (() if final is None else tuple(final)),
                    4 * product,
                    place=(pair_rows, pair),
                    aliased=final is not None,
                )
            elif power:
                shapes = [sds(pair_rows, width, BF16)]
                if pair == 1:
                    shapes += [sds(points, piece, t) for piece in pieces for t in (F32, BF16)]
                else:
                    shapes += [sds(points, width, F32)]
                out = call(
                    functools.partial(edge_sum_body, pair, at, sums is None),
                    shapes,
                    (*args, own, *(sums or [])),
                    5 * product,
                )
                m_next[pair], sums = (out[0], 0), list(out[1:])
            else:
                (out,) = call(
                    functools.partial(edge_body, pair, at),
                    [sds(pair_rows, width, BF16)],
                    args,
                    4 * product,
                )
                m_next[pair] = (out, 0)
        m, m_parts = None, m_next
    return (final[0][None, None], share_h[None])


def solution(mesh):
    in_specs = (
        P("row", "col", None, None),
        P("row", "col", None),
        P("row", "col", None, None),
        P("col", "row", None),
        P(),
        P(),
        P(),
    )
    out_specs = (P("row", "col", None, None), P("col", "row", None))
    return jax.shard_map(shards, mesh=mesh, in_specs=in_specs, out_specs=out_specs, check_vma=False)
```

```python
import functools
import math

import jax
import jax.numpy as jnp
from jax import lax
from jax.experimental import pallas as pl
from jax.experimental.pallas import tpu as pltpu
from jax.sharding import PartitionSpec as P


OFFSETS = (0, 0, 1, -1, 2, -2, 3, -3)
ROOT_HALF = 0.7071067811865476
PAIRS = len(OFFSETS) // 2
F32 = jnp.float32
BF16 = jnp.bfloat16


def dot(a, b):
    return jnp.dot(a, b, preferred_element_type=F32)


def silu(v):
    half = 0.5 * v
    return half + half * jnp.tanh(half)


def call(body, outs, args, flops, spaces={}, out_space=pltpu.VMEM, scratch=(), limit=32 << 20, aliases={}):
    moved = sum(math.prod(a.shape) * a.dtype.itemsize for a in list(args) + list(outs))
    return pl.pallas_call(
        body,
        out_shape=tuple(jax.ShapeDtypeStruct(o.shape, o.dtype) for o in outs),
        in_specs=[
            pl.BlockSpec(memory_space=spaces.get(i, pltpu.VMEM)) for i in range(len(args))
        ],
        out_specs=tuple(pl.BlockSpec(memory_space=out_space) for _ in outs),
        scratch_shapes=list(scratch),
        input_output_aliases=aliases,
        compiler_params=pltpu.CompilerParams(vmem_limit_bytes=limit),
        cost_estimate=pl.CostEstimate(flops=flops, bytes_accessed=moved, transcendentals=0),
    )(*args)


def partner_numbers(targets, me, share):
    return ((targets // share) ^ me) * share + targets % share


def hot_rows(targets, first, count):
    points = lax.broadcasted_iota(jnp.int32, (count, targets.shape[1]), 0) + first
    return (points == targets).astype(F32).astype(BF16)


def joined(refs):
    if len(refs) == 1:
        return refs[0][...]
    return jnp.concatenate([ref[...] for ref in refs], axis=0)


def placed(order_ref, k):
    block = order_ref.shape[1]
    place = lax.broadcasted_iota(jnp.int32, (block, block), 0)
    return (place == order_ref[k : k + 1, :]).astype(F32).astype(BF16)


def split_columns(total, outs):
    at = 0
    for exact, sent in zip(outs[::2], outs[1::2]):
        piece = total[:, at : at + exact.shape[1]]
        exact[...] = piece
        sent[...] = piece.astype(BF16)
        at += exact.shape[1]


def partial_body(targets_ref, m_ref, *outs):
    split_columns(sums_of(targets_ref, 0, m_ref[...], outs[0].shape[0]), outs)


def swapped(ref, bit, share):
    count = ref.shape[0] // share
    parts = [ref[(k ^ bit) * share : (k ^ bit) * share + share, :] for k in range(count)]
    return jnp.concatenate(parts, axis=0).astype(F32)


def add_body(bits, share, *refs):
    count = len(bits)
    for p, bit in enumerate(bits):
        total = refs[p][...] + swapped(refs[count + p], bit, share)
        refs[2 * count + 2 * p][...] = total
        refs[2 * count + 2 * p + 1][...] = total.astype(BF16)


def update_body(bits, share, scale, w_ref, *refs):
    count = len(bits)
    nodes, table_ref = refs[2 * count : -1], refs[-1]
    totals = [refs[p][...] + swapped(refs[count + p], bit, share) for p, bit in enumerate(bits)]
    z = (jnp.concatenate(totals, axis=1) * scale).astype(BF16)
    table_ref[...] = (joined(nodes).astype(F32) + silu(dot(z, w_ref[...]))).astype(BF16)


def order_body(order_ref, hot_ref, out):
    block = order_ref.shape[1]
    for k in range(out.shape[0] // block):
        rows = pl.ds(k * block, block)
        out[rows, :] = dot(placed(order_ref, k), hot_ref[rows, :]).astype(BF16)


def pre_body(layer, order_ref, *refs):
    (w_ref, w_node_ref, out, w_node_out), at = refs[-4:], 0
    w_node_out[...] = w_node_ref[layer]
    block = order_ref.shape[1]
    for ref in refs[:-4]:
        rows = min(ref.shape[0], out.shape[0] - at)
        width = ref.shape[1]
        m_rows = [
            dot(placed(order_ref, (at + i) // block), ref[i : i + block, :]).astype(BF16)
            for i in range(0, rows, block)
        ]
        out[at : at + rows, :] = dot(jnp.concatenate(m_rows, axis=0), w_ref[layer, :width, :])
        at += rows


def sent_rows(k, block, hot_ref, pre_ref, table, w):
    rows = pl.ds(k * block, block)
    h_rows = dot(hot_ref[rows, :], table).astype(BF16)
    return (pre_ref[rows, :] + dot(h_rows, w)).astype(BF16)


def send_body(layer, first, hot_ref, pre_ref, w_ref, table_ref, *outs):
    block, width = outs[0].shape
    table = table_ref[...]
    w = w_ref[layer, width : 2 * width, :]
    for half, out in enumerate(outs):
        out[...] = sent_rows(first + half, block, hot_ref, pre_ref, table, w)


def edge_blocks(layer, got, m_blocks, w_ref):
    x1 = [silu(g).astype(BF16) for g in got]
    a1 = [silu(dot(x, w_ref[layer, 0, 0])).astype(BF16) for x in x1]
    x2 = [
        ((x.astype(F32) + silu(dot(a, w_ref[layer, 0, 1]))) * ROOT_HALF).astype(BF16)
        for x, a in zip(x1, a1)
    ]
    a2 = [silu(dot(x, w_ref[layer, 1, 0])).astype(BF16) for x in x2]
    for old, x, a in zip(m_blocks, x2, a2):
        x3 = (x.astype(F32) + silu(dot(a, w_ref[layer, 1, 1]))) * ROOT_HALF
        yield ((old.astype(F32) + x3) * ROOT_HALF).astype(BF16)


def sums_of(targets_ref, first, new, points):
    return dot(hot_rows(targets_ref[:, first : first + new.shape[0]], 0, points), new)


def local_body(layer, last, hot_ref, sent_ref, pre_ref, table_ref, m_ref, w_in_ref, w_ref, *refs):
    part_ref, new_ref, third_ref = refs[-3:]
    width, local = m_ref.shape[1], new_ref.shape[0]
    block = local // 2
    table = table_ref[...]
    w_mid, w_end = w_in_ref[layer, width : 2 * width, :], w_in_ref[layer, 2 * width :, :]
    got, old = [], []
    for k in range(2):
        rows = slice(k * block, (k + 1) * block)
        h_tgt = dot(hot_ref[rows, :], table).astype(BF16)
        received = sent_rows(k ^ 1, block, sent_ref, pre_ref, table, w_mid)
        got.append(received.astype(F32) + dot(h_tgt, w_end))
        old.append(m_ref[rows, :])
    for k, new in enumerate(edge_blocks(layer, got, old, w_ref)):
        new_ref[k * block : (k + 1) * block, :] = new
    h_tgt = dot(hot_ref[local:, :], table).astype(BF16)
    part_ref[...] = dot(h_tgt, w_end)
    if last:
        third_ref[...] = table_ref[: third_ref.shape[0], :]
    else:
        third_ref[...] = sums_of(refs[0], 0, new_ref[...], third_ref.shape[0])


def new_rows(layer, m_at, part_at, part_ref, m_ref, w_ref, got_refs):
    got, old = [], []
    for i, ref in enumerate(got_refs):
        size = ref.shape[0]
        rows = slice(part_at + i * size, part_at + (i + 1) * size)
        got.append(ref[...].astype(F32) + part_ref[rows, :])
        old.append(m_ref[m_at + i * size : m_at + (i + 1) * size, :])
    return edge_blocks(layer, got, old, w_ref)


def edge_body(
    layer, at, first, part_at, count, part_ref, m_ref, w_ref, targets_ref, sum_ref, *refs
):
    got, new_ref, sums = refs[:count], refs[count], refs[count + 1 :]
    size = got[0].shape[0]
    for i, new in enumerate(new_rows(layer, at, part_at, part_ref, m_ref, w_ref, got)):
        new_ref[i * size : (i + 1) * size, :] = new
    total = sum_ref[...] + sums_of(targets_ref, first, new_ref[...], sum_ref.shape[0])
    if len(sums) == 1:
        sums[0][...] = total
    else:
        split_columns(total, sums)


def last_body(layer, at, first, part_at, count, part_ref, m_ref, w_ref, *refs):
    got, done_ref = refs[:count], refs[count]
    out, rows_ref, sems = refs[-3:]
    size = got[0].shape[0]
    copies = []
    if len(done_ref.shape) == 2 and done_ref.shape[0] == first:
        copies.append(pltpu.make_async_copy(done_ref, out.at[pl.ds(0, first), :], sems.at[count]))
        copies[0].start()
    for i, new in enumerate(new_rows(layer, at, part_at, part_ref, m_ref, w_ref, got)):
        rows = pl.ds(i * size, size)
        rows_ref[rows, :] = new
        target = out.at[pl.ds(first + i * size, size), :]
        copies.append(pltpu.make_async_copy(rows_ref.at[rows, :], target, sems.at[i]))
        copies[-1].start()
    for copy in copies:
        copy.wait()


def row_move(value, bit):
    count = lax.axis_size("row")
    return lax.ppermute(value, "row", [(s, s ^ bit) for s in range(count)])


def col_shift(value, steps):
    count = lax.axis_size("col")
    return lax.ppermute(value, "col", [(s, (s + steps) % count) for s in range(count)])


def column_pieces(width, count):
    lanes = width // 128
    sizes = [lanes // count + (p < lanes % count) for p in range(count)]
    return [128 * size for size in sizes]


def sds(rows, width, dtype):
    return jax.ShapeDtypeStruct((rows, width), dtype)


def shards(messages, targets, reverse_rows, nodes, w_in, w_res, w_node):
    m = messages[0, 0]
    order = reverse_rows[0, 0]
    share_h = nodes[0]
    edges, width = m.shape
    share = share_h.shape[0]
    blocks, block = order.shape
    pair_rows = 2 * block
    count = lax.axis_size("row")
    assert count & (count - 1) == 0
    points = count * share
    scale = 1.0 / math.sqrt(edges // share)
    me = lax.axis_index("row").astype(jnp.int32)
    layers = w_in.shape[0]
    product = 2 * pair_rows * width * width
    rounds = count.bit_length() - 1
    pieces = column_pieces(width, rounds)
    piece_shapes = [sds(points, piece, t) for piece in pieces for t in (F32, BF16)]
    own = partner_numbers(targets[0], me, share)
    table = [share_h]
    sums = call(partial_body, piece_shapes, (own, m), 2 * points * edges * width)
    for k in range(1, count):
        table.append(row_move(share_h, k))
    hot = (own[0][:, None] == jnp.arange(points, dtype=jnp.int32)[None, :]).astype(BF16)
    groups = (tuple(range(2, blocks - 2)), tuple(range(blocks - 2, blocks)))
    m_parts = [(m, 0)] + [(m, ks[0] * block) for ks in groups]
    for layer in range(layers):
        first, last = layer == 0, layer == layers - 1
        for r in range(rounds):
            bits = [1 << ((p + r) % rounds) for p in range(rounds)]
            got = []
            for p, bit in enumerate(bits):
                got.append(row_move(sums[2 * p + 1], bit))
            if r < rounds - 1:
                sums = call(
                    functools.partial(add_body, bits, share),
                    piece_shapes,
                    (*sums[::2], *got),
                    points * width,
                )
        if first:
            (hot_sent,) = call(
                order_body,
                [sds(edges, points, BF16)],
                (order, hot),
                2 * edges * block * points,
            )
        pre, w_point = call(
            functools.partial(pre_body, layer),
            [sds(edges, width, F32), sds(width, width, BF16)],
            (order, *((m,) if first else [part for part, _ in m_parts]), w_in, w_node),
            PAIRS * product,
        )
        (h,) = call(
            functools.partial(update_body, bits, share, scale),
            [sds(points, width, BF16)],
            (w_point, *sums[::2], *got, *table),
            2 * points * width * width,
        )
        table = [h]
        sent = {}
        for pair in (2, 1, 3):
            outs = call(
                functools.partial(send_body, layer, 2 * pair),
                [sds(block, width, BF16)] * 2,
                (hot_sent, pre, w_in, h),
                2 * product,
            )
            for half, out in enumerate(outs):
                k = 2 * pair + half
                sent[k ^ 1] = col_shift(out, OFFSETS[k])
        out = call(
            functools.partial(local_body, layer, last),
            [sds(edges - pair_rows, width, F32), sds(pair_rows, width, BF16)]
            + [sds(share, width, BF16) if last else sds(points, width, F32)],
            (hot, hot_sent, pre, h, m_parts[0][0], w_in, w_res) + (() if last else (own,)),
            12 * product,
        )
        part, done, sums = out[0], [out[1]], [out[2]]
        if last:
            share_h = out[2]
        for name, ks, (source, at) in zip(("near", "far"), groups, m_parts[1:]):
            where = (layer, at, ks[0] * block, ks[0] * block - pair_rows, len(ks))
            got = [sent[k] for k in ks]
            if last:
                done = call(
                    functools.partial(last_body, *where),
                    [sds(edges, width, BF16)],
                    (part, source, w_res, *got, *done),
                    2 * len(ks) * product,
                    spaces={3 + len(ks): pltpu.HBM} if name == "far" else {},
                    out_space=pltpu.HBM,
                    scratch=(
                        pltpu.VMEM((len(ks) * block, width), BF16),
                        pltpu.SemaphoreType.DMA((len(ks) + 1,)),
                    ),
                    aliases={3 + len(ks): 0} if name == "far" else {},
                )
            else:
                new, *sums = call(
                    functools.partial(edge_body, *where),
                    [sds(len(ks) * block, width, BF16)]
                    + (piece_shapes if name == "far" else [sds(points, width, F32)]),
                    (part, source, w_res, own, *sums, *got),
                    3 * len(ks) * product,
                )
                done.append(new)
        m_parts = [(new, 0) for new in done]
    return (done[0][None, None], share_h[None])


def solution(mesh):
    in_specs = (
        P("row", "col", None, None),
        P("row", "col", None),
        P("row", "col", None, None),
        P("col", "row", None),
        P(),
        P(),
        P(),
    )
    out_specs = (P("row", "col", None, None), P("col", "row", None))
    return jax.shard_map(shards, mesh=mesh, in_specs=in_specs, out_specs=out_specs, check_vma=False)
```

```python
import functools
import math

import jax
import jax.numpy as jnp
from jax import lax
from jax.experimental import pallas as pl
from jax.experimental.pallas import tpu as pltpu
from jax.sharding import PartitionSpec as P


OFFSETS = (0, 0, 1, -1, 2, -2, 3, -3)
ROOT_HALF = 0.7071067811865476
PAIRS = len(OFFSETS) // 2
F32 = jnp.float32
BF16 = jnp.bfloat16


def dot(a, b):
    return jnp.dot(a, b, preferred_element_type=F32)


def silu(v):
    half = 0.5 * v
    return half + half * jnp.tanh(half)


def call(body, outs, args, flops, spaces={}, out_space=pltpu.VMEM, scratch=(), limit=32 << 20, aliases={}):
    moved = sum(math.prod(a.shape) * a.dtype.itemsize for a in list(args) + list(outs))
    return pl.pallas_call(
        body,
        out_shape=tuple(jax.ShapeDtypeStruct(o.shape, o.dtype) for o in outs),
        in_specs=[
            pl.BlockSpec(memory_space=spaces.get(i, pltpu.VMEM)) for i in range(len(args))
        ],
        out_specs=tuple(pl.BlockSpec(memory_space=out_space) for _ in outs),
        scratch_shapes=list(scratch),
        input_output_aliases=aliases,
        compiler_params=pltpu.CompilerParams(vmem_limit_bytes=limit),
        cost_estimate=pl.CostEstimate(flops=flops, bytes_accessed=moved, transcendentals=0),
    )(*args)


def partner_numbers(targets, me, share):
    return ((targets // share) ^ me) * share + targets % share


def hot_rows(targets, first, count):
    points = lax.broadcasted_iota(jnp.int32, (count, targets.shape[1]), 0) + first
    return (points == targets).astype(F32).astype(BF16)


def joined(refs):
    if len(refs) == 1:
        return refs[0][...]
    return jnp.concatenate([ref[...] for ref in refs], axis=0)


def placed(order_ref, k):
    block = order_ref.shape[1]
    place = lax.broadcasted_iota(jnp.int32, (block, block), 0)
    return (place == order_ref[k : k + 1, :]).astype(F32).astype(BF16)


def split_columns(total, outs):
    at = 0
    for exact, sent in zip(outs[::2], outs[1::2]):
        piece = total[:, at : at + exact.shape[1]]
        exact[...] = piece
        sent[...] = piece.astype(BF16)
        at += exact.shape[1]


def partial_body(targets_ref, m_ref, m_out, *outs):
    m_out[...] = m_ref[...]
    split_columns(sums_of(targets_ref, 0, m_ref[...], outs[0].shape[0]), outs)


def swapped(ref, bit, share):
    count = ref.shape[0] // share
    parts = [ref[(k ^ bit) * share : (k ^ bit) * share + share, :] for k in range(count)]
    return jnp.concatenate(parts, axis=0).astype(F32)


def add_body(bits, share, *refs):
    count = len(bits)
    for p, bit in enumerate(bits):
        total = refs[p][...] + swapped(refs[count + p], bit, share)
        refs[2 * count + 2 * p][...] = total
        refs[2 * count + 2 * p + 1][...] = total.astype(BF16)


def update_body(bits, share, scale, w_ref, *refs):
    count = len(bits)
    nodes, table_ref = refs[2 * count : -1], refs[-1]
    totals = [refs[p][...] + swapped(refs[count + p], bit, share) for p, bit in enumerate(bits)]
    z = (jnp.concatenate(totals, axis=1) * scale).astype(BF16)
    table_ref[...] = (joined(nodes).astype(F32) + silu(dot(z, w_ref[...]))).astype(BF16)


def order_body(order_ref, hot_ref, out):
    block = order_ref.shape[1]
    for k in range(out.shape[0] // block):
        rows = pl.ds(k * block, block)
        out[rows, :] = dot(placed(order_ref, k), hot_ref[rows, :]).astype(BF16)


def pre_body(layer, order_ref, *refs):
    (w_ref, out), at = refs[-2:], 0
    block = order_ref.shape[1]
    for ref in refs[:-2]:
        rows = min(ref.shape[0], out.shape[0] - at)
        width = ref.shape[1]
        m_rows = [
            dot(placed(order_ref, (at + i) // block), ref[i : i + block, :]).astype(BF16)
            for i in range(0, rows, block)
        ]
        out[at : at + rows, :] = dot(jnp.concatenate(m_rows, axis=0), w_ref[layer, :width, :])
        at += rows


def sent_rows(k, block, hot_ref, pre_ref, table, w):
    rows = pl.ds(k * block, block)
    h_rows = dot(hot_ref[rows, :], table).astype(BF16)
    return (pre_ref[rows, :] + dot(h_rows, w)).astype(BF16)


def send_body(layer, first, hot_ref, pre_ref, w_ref, table_ref, *outs):
    block, width = outs[0].shape
    table = table_ref[...]
    w = w_ref[layer, width : 2 * width, :]
    rows = [pl.ds((first + half) * block, block) for half in range(2)]
    h_rows = [dot(hot_ref[r, :], table).astype(BF16) for r in rows]
    for r, h, out in zip(rows, h_rows, outs):
        out[...] = (pre_ref[r, :] + dot(h, w)).astype(BF16)


def edge_blocks(layer, got, m_blocks, w_ref):
    x1 = [silu(g).astype(BF16) for g in got]
    a1 = [silu(dot(x, w_ref[layer, 0, 0])).astype(BF16) for x in x1]
    x2 = [
        ((x.astype(F32) + silu(dot(a, w_ref[layer, 0, 1]))) * ROOT_HALF).astype(BF16)
        for x, a in zip(x1, a1)
    ]
    a2 = [silu(dot(x, w_ref[layer, 1, 0])).astype(BF16) for x in x2]
    for old, x, a in zip(m_blocks, x2, a2):
        x3 = (x.astype(F32) + silu(dot(a, w_ref[layer, 1, 1]))) * ROOT_HALF
        yield ((old.astype(F32) + x3) * ROOT_HALF).astype(BF16)


def sums_of(targets_ref, first, new, points):
    return dot(hot_rows(targets_ref[:, first : first + new.shape[0]], 0, points), new)


def local_body(layer, last, hot_ref, sent_ref, pre_ref, table_ref, m_ref, w_in_ref, w_ref, *refs):
    part_ref, new_ref, third_ref = refs[-3:]
    width, local = m_ref.shape[1], new_ref.shape[0]
    block = local // 2
    table = table_ref[...]
    w_mid, w_end = w_in_ref[layer, width : 2 * width, :], w_in_ref[layer, 2 * width :, :]
    got, old = [], []
    for k in range(2):
        rows = slice(k * block, (k + 1) * block)
        h_tgt = dot(hot_ref[rows, :], table).astype(BF16)
        received = sent_rows(k ^ 1, block, sent_ref, pre_ref, table, w_mid)
        got.append(received.astype(F32) + dot(h_tgt, w_end))
        old.append(m_ref[rows, :])
    for k, new in enumerate(edge_blocks(layer, got, old, w_ref)):
        new_ref[k * block : (k + 1) * block, :] = new
    h_tgt = dot(hot_ref[local:, :], table).astype(BF16)
    part_ref[...] = dot(h_tgt, w_end)
    if last:
        third_ref[...] = table_ref[: third_ref.shape[0], :]
    else:
        third_ref[...] = sums_of(refs[0], 0, new_ref[...], third_ref.shape[0])


def new_rows(layer, m_at, part_at, part_ref, m_ref, w_ref, got_refs):
    got, old = [], []
    for i, ref in enumerate(got_refs):
        size = ref.shape[0]
        rows = slice(part_at + i * size, part_at + (i + 1) * size)
        got.append(ref[...].astype(F32) + part_ref[rows, :])
        old.append(m_ref[m_at + i * size : m_at + (i + 1) * size, :])
    return edge_blocks(layer, got, old, w_ref)


def edge_body(
    layer, at, first, part_at, count, part_ref, m_ref, w_ref, targets_ref, sum_ref, *refs
):
    got, new_ref, sums = refs[:count], refs[count], refs[count + 1 :]
    size = got[0].shape[0]
    for i, new in enumerate(new_rows(layer, at, part_at, part_ref, m_ref, w_ref, got)):
        new_ref[i * size : (i + 1) * size, :] = new
    total = sum_ref[...] + sums_of(targets_ref, first, new_ref[...], sum_ref.shape[0])
    if len(sums) == 1:
        sums[0][...] = total
    else:
        split_columns(total, sums)


def last_body(layer, at, first, part_at, count, part_ref, m_ref, w_ref, *refs):
    got, done_ref = refs[:count], refs[count]
    out, rows_ref, sems = refs[-3:]
    size = got[0].shape[0]
    copies = []
    if len(done_ref.shape) == 2 and done_ref.shape[0] == first:
        copies.append(pltpu.make_async_copy(done_ref, out.at[pl.ds(0, first), :], sems.at[count]))
        copies[0].start()
    for i, new in enumerate(new_rows(layer, at, part_at, part_ref, m_ref, w_ref, got)):
        rows = pl.ds(i * size, size)
        rows_ref[rows, :] = new
        target = out.at[pl.ds(first + i * size, size), :]
        copies.append(pltpu.make_async_copy(rows_ref.at[rows, :], target, sems.at[i]))
        copies[-1].start()
    for copy in copies:
        copy.wait()


def row_move(value, bit):
    count = lax.axis_size("row")
    return lax.ppermute(value, "row", [(s, s ^ bit) for s in range(count)])


def col_shift(value, steps):
    count = lax.axis_size("col")
    return lax.ppermute(value, "col", [(s, (s + steps) % count) for s in range(count)])


def column_pieces(width, count):
    lanes = width // 128
    sizes = [lanes // count + (p < lanes % count) for p in range(count)]
    return [128 * size for size in sizes]


def sds(rows, width, dtype):
    return jax.ShapeDtypeStruct((rows, width), dtype)


def shards(messages, targets, reverse_rows, nodes, w_in, w_res, w_node):
    m = messages[0, 0]
    order = reverse_rows[0, 0]
    share_h = nodes[0]
    edges, width = m.shape
    share = share_h.shape[0]
    blocks, block = order.shape
    pair_rows = 2 * block
    count = lax.axis_size("row")
    assert count & (count - 1) == 0
    points = count * share
    scale = 1.0 / math.sqrt(edges // share)
    me = lax.axis_index("row").astype(jnp.int32)
    layers = w_in.shape[0]
    product = 2 * pair_rows * width * width
    rounds = count.bit_length() - 1
    pieces = column_pieces(width, rounds)
    piece_shapes = [sds(points, piece, t) for piece in pieces for t in (F32, BF16)]
    own = partner_numbers(targets[0], me, share)
    table = [share_h]
    m, *sums = call(
        partial_body,
        [sds(edges, width, BF16)] + piece_shapes,
        (own, m),
        2 * points * edges * width,
    )
    w_in, w_res, w_node, order, *sums = lax.optimization_barrier(
        (w_in, w_res, w_node, order, *sums)
    )
    for k in range(1, count):
        table.append(row_move(share_h, k))
    hot = (own[0][:, None] == jnp.arange(points, dtype=jnp.int32)[None, :]).astype(BF16)
    groups = (tuple(range(2, blocks - 2)), tuple(range(blocks - 2, blocks)))
    m_parts = [(m, 0)] + [(m, ks[0] * block) for ks in groups]
    for layer in range(layers):
        first, last = layer == 0, layer == layers - 1
        for r in range(rounds):
            bits = [1 << ((p + r) % rounds) for p in range(rounds)]
            got = []
            for p, bit in enumerate(bits):
                got.append(row_move(sums[2 * p + 1], bit))
            if r < rounds - 1:
                sums = call(
                    functools.partial(add_body, bits, share),
                    piece_shapes,
                    (*sums[::2], *got),
                    points * width,
                )
        if first:
            (hot_sent,) = call(
                order_body,
                [sds(edges, points, BF16)],
                (order, hot),
                2 * edges * block * points,
            )
        (pre,) = call(
            functools.partial(pre_body, layer),
            [sds(edges, width, F32)],
            (order, *((m,) if first else [part for part, _ in m_parts]), w_in),
            PAIRS * product,
        )
        (h,) = call(
            functools.partial(update_body, bits, share, scale),
            [sds(points, width, BF16)],
            (w_node[layer], *sums[::2], *got, *table),
            2 * points * width * width,
        )
        table = [h]
        sent = {}
        for pair in (2, 1, 3):
            outs = call(
                functools.partial(send_body, layer, 2 * pair),
                [sds(block, width, BF16)] * 2,
                (hot_sent, pre, w_in, h),
                2 * product,
            )
            for half, out in enumerate(outs):
                k = 2 * pair + half
                sent[k ^ 1] = col_shift(out, OFFSETS[k])
        out = call(
            functools.partial(local_body, layer, last),
            [sds(edges - pair_rows, width, F32), sds(pair_rows, width, BF16)]
            + [sds(share, width, BF16) if last else sds(points, width, F32)],
            (hot, hot_sent, pre, h, m_parts[0][0], w_in, w_res) + (() if last else (own,)),
            12 * product,
        )
        part, done, sums = out[0], [out[1]], [out[2]]
        if last:
            share_h = out[2]
        for name, ks, (source, at) in zip(("near", "far"), groups, m_parts[1:]):
            where = (layer, at, ks[0] * block, ks[0] * block - pair_rows, len(ks))
            got = [sent[k] for k in ks]
            if last:
                done = call(
                    functools.partial(last_body, *where),
                    [sds(edges, width, BF16)],
                    (part, source, w_res, *got, *done),
                    2 * len(ks) * product,
                    spaces={3 + len(ks): pltpu.HBM} if name == "far" else {},
                    out_space=pltpu.HBM,
                    scratch=(
                        pltpu.VMEM((len(ks) * block, width), BF16),
                        pltpu.SemaphoreType.DMA((len(ks) + 1,)),
                    ),
                    aliases={3 + len(ks): 0} if name == "far" else {},
                )
            else:
                new, *sums = call(
                    functools.partial(edge_body, *where),
                    [sds(len(ks) * block, width, BF16)]
                    + (piece_shapes if name == "far" else [sds(points, width, F32)]),
                    (part, source, w_res, own, *sums, *got),
                    3 * len(ks) * product,
                )
                done.append(new)
        m_parts = [(new, 0) for new in done]
    return (done[0][None, None], share_h[None])


def solution(mesh):
    in_specs = (
        P("row", "col", None, None),
        P("row", "col", None),
        P("row", "col", None, None),
        P("col", "row", None),
        P(),
        P(),
        P(),
    )
    out_specs = (P("row", "col", None, None), P("col", "row", None))
    return jax.shard_map(shards, mesh=mesh, in_specs=in_specs, out_specs=out_specs, check_vma=False)
```

```python
import functools
import math

import jax
import jax.numpy as jnp
from jax import lax
from jax.experimental import pallas as pl
from jax.experimental.pallas import tpu as pltpu
from jax.sharding import PartitionSpec as P


OFFSETS = (0, 0, 1, -1, 2, -2, 3, -3)
ROOT_HALF = 0.7071067811865476
PAIRS = len(OFFSETS) // 2
F32 = jnp.float32
BF16 = jnp.bfloat16


def dot(a, b):
    return jnp.dot(a, b, preferred_element_type=F32)


def silu(v):
    half = 0.5 * v
    return half + half * jnp.tanh(half)


def call(body, outs, args, flops, spaces={}, out_space=pltpu.VMEM, scratch=(), limit=32 << 20, aliases={}):
    moved = sum(math.prod(a.shape) * a.dtype.itemsize for a in list(args) + list(outs))
    return pl.pallas_call(
        body,
        out_shape=tuple(jax.ShapeDtypeStruct(o.shape, o.dtype) for o in outs),
        in_specs=[
            pl.BlockSpec(memory_space=spaces.get(i, pltpu.VMEM)) for i in range(len(args))
        ],
        out_specs=tuple(pl.BlockSpec(memory_space=out_space) for _ in outs),
        scratch_shapes=list(scratch),
        input_output_aliases=aliases,
        compiler_params=pltpu.CompilerParams(vmem_limit_bytes=limit),
        cost_estimate=pl.CostEstimate(flops=flops, bytes_accessed=moved, transcendentals=0),
    )(*args)


def partner_numbers(targets, me, share):
    return ((targets // share) ^ me) * share + targets % share


def hot_rows(targets, first, count):
    points = lax.broadcasted_iota(jnp.int32, (count, targets.shape[1]), 0) + first
    return (points == targets).astype(F32).astype(BF16)


def joined(refs):
    if len(refs) == 1:
        return refs[0][...]
    return jnp.concatenate([ref[...] for ref in refs], axis=0)


def placed(order_ref, k):
    block = order_ref.shape[1]
    place = lax.broadcasted_iota(jnp.int32, (block, block), 0)
    return (place == order_ref[k : k + 1, :]).astype(F32).astype(BF16)


def split_columns(total, outs):
    at = 0
    for exact, sent in zip(outs[::2], outs[1::2]):
        piece = total[:, at : at + exact.shape[1]]
        exact[...] = piece
        sent[...] = piece.astype(BF16)
        at += exact.shape[1]


def partial_body(targets_ref, m_ref, m_out, *outs):
    m_out[...] = m_ref[...]
    split_columns(sums_of(targets_ref, 0, m_ref[...], outs[0].shape[0]), outs)


def swapped(ref, bit, share):
    count = ref.shape[0] // share
    parts = [ref[(k ^ bit) * share : (k ^ bit) * share + share, :] for k in range(count)]
    return jnp.concatenate(parts, axis=0).astype(F32)


def add_body(bits, share, *refs):
    count = len(bits)
    for p, bit in enumerate(bits):
        total = refs[p][...] + swapped(refs[count + p], bit, share)
        refs[2 * count + 2 * p][...] = total
        refs[2 * count + 2 * p + 1][...] = total.astype(BF16)


def update_body(bits, share, scale, layer, at, w_ref, hot_ref, pre_ref, w_in_ref, *refs):
    count = len(bits)
    nodes, (table_ref, *outs) = refs[2 * count : -3], refs[-3:]
    totals = [refs[p][...] + swapped(refs[count + p], bit, share) for p, bit in enumerate(bits)]
    z = (jnp.concatenate(totals, axis=1) * scale).astype(BF16)
    table = (joined(nodes).astype(F32) + silu(dot(z, w_ref[...]))).astype(BF16)
    table_ref[...] = table
    send_rows(layer, at, hot_ref, pre_ref, w_in_ref, table, outs)


def order_body(order_ref, hot_ref, out):
    block = order_ref.shape[1]
    for k in range(out.shape[0] // block):
        rows = pl.ds(k * block, block)
        out[rows, :] = dot(placed(order_ref, k), hot_ref[rows, :]).astype(BF16)


def pre_body(layer, order_ref, *refs):
    (w_ref, out), at = refs[-2:], 0
    block = order_ref.shape[1]
    for ref in refs[:-2]:
        rows = min(ref.shape[0], out.shape[0] - at)
        width = ref.shape[1]
        m_rows = [
            dot(placed(order_ref, (at + i) // block), ref[i : i + block, :]).astype(BF16)
            for i in range(0, rows, block)
        ]
        out[at : at + rows, :] = dot(jnp.concatenate(m_rows, axis=0), w_ref[layer, :width, :])
        at += rows


def sent_rows(k, block, hot_ref, pre_ref, table, w):
    rows = pl.ds(k * block, block)
    h_rows = dot(hot_ref[rows, :], table).astype(BF16)
    return (pre_ref[rows, :] + dot(h_rows, w)).astype(BF16)


def send_rows(layer, first, hot_ref, pre_ref, w_ref, table, outs):
    block, width = outs[0].shape
    w = w_ref[layer, width : 2 * width, :]
    rows = [pl.ds((first + half) * block, block) for half in range(2)]
    h_rows = [dot(hot_ref[r, :], table).astype(BF16) for r in rows]
    for r, h, out in zip(rows, h_rows, outs):
        out[...] = (pre_ref[r, :] + dot(h, w)).astype(BF16)


def send_body(layer, first, hot_ref, pre_ref, w_ref, table_ref, *outs):
    send_rows(layer, first, hot_ref, pre_ref, w_ref, table_ref[...], outs)


def edge_blocks(layer, got, m_blocks, w_ref):
    x1 = [silu(g).astype(BF16) for g in got]
    a1 = [silu(dot(x, w_ref[layer, 0, 0])).astype(BF16) for x in x1]
    x2 = [
        ((x.astype(F32) + silu(dot(a, w_ref[layer, 0, 1]))) * ROOT_HALF).astype(BF16)
        for x, a in zip(x1, a1)
    ]
    a2 = [silu(dot(x, w_ref[layer, 1, 0])).astype(BF16) for x in x2]
    for old, x, a in zip(m_blocks, x2, a2):
        x3 = (x.astype(F32) + silu(dot(a, w_ref[layer, 1, 1]))) * ROOT_HALF
        yield ((old.astype(F32) + x3) * ROOT_HALF).astype(BF16)


def sums_of(targets_ref, first, new, points):
    return dot(hot_rows(targets_ref[:, first : first + new.shape[0]], 0, points), new)


def local_body(layer, last, hot_ref, sent_ref, pre_ref, table_ref, m_ref, w_in_ref, w_ref, *refs):
    part_ref, new_ref, third_ref = refs[-3:]
    width, local = m_ref.shape[1], new_ref.shape[0]
    block = local // 2
    table = table_ref[...]
    w_mid, w_end = w_in_ref[layer, width : 2 * width, :], w_in_ref[layer, 2 * width :, :]
    got, old = [], []
    for k in range(2):
        rows = slice(k * block, (k + 1) * block)
        h_tgt = dot(hot_ref[rows, :], table).astype(BF16)
        received = sent_rows(k ^ 1, block, sent_ref, pre_ref, table, w_mid)
        got.append(received.astype(F32) + dot(h_tgt, w_end))
        old.append(m_ref[rows, :])
    for k, new in enumerate(edge_blocks(layer, got, old, w_ref)):
        new_ref[k * block : (k + 1) * block, :] = new
    h_tgt = dot(hot_ref[local:, :], table).astype(BF16)
    part_ref[...] = dot(h_tgt, w_end)
    if last:
        third_ref[...] = table_ref[: third_ref.shape[0], :]
    else:
        third_ref[...] = sums_of(refs[0], 0, new_ref[...], third_ref.shape[0])


def new_rows(layer, m_at, part_at, part_ref, m_ref, w_ref, got_refs):
    got, old = [], []
    for i, ref in enumerate(got_refs):
        size = ref.shape[0]
        rows = slice(part_at + i * size, part_at + (i + 1) * size)
        got.append(ref[...].astype(F32) + part_ref[rows, :])
        old.append(m_ref[m_at + i * size : m_at + (i + 1) * size, :])
    return edge_blocks(layer, got, old, w_ref)


def edge_body(
    layer, at, first, part_at, count, part_ref, m_ref, w_ref, targets_ref, sum_ref, *refs
):
    got, new_ref, sums = refs[:count], refs[count], refs[count + 1 :]
    size = got[0].shape[0]
    for i, new in enumerate(new_rows(layer, at, part_at, part_ref, m_ref, w_ref, got)):
        new_ref[i * size : (i + 1) * size, :] = new
    total = sum_ref[...] + sums_of(targets_ref, first, new_ref[...], sum_ref.shape[0])
    if len(sums) == 1:
        sums[0][...] = total
    else:
        split_columns(total, sums)


def last_body(layer, at, first, part_at, count, part_ref, m_ref, w_ref, *refs):
    got, done_ref = refs[:count], refs[count]
    out, rows_ref, sems = refs[-3:]
    size = got[0].shape[0]
    copies = []
    if len(done_ref.shape) == 2 and done_ref.shape[0] == first:
        copies.append(pltpu.make_async_copy(done_ref, out.at[pl.ds(0, first), :], sems.at[count]))
        copies[0].start()
    for i, new in enumerate(new_rows(layer, at, part_at, part_ref, m_ref, w_ref, got)):
        rows = pl.ds(i * size, size)
        rows_ref[rows, :] = new
        target = out.at[pl.ds(first + i * size, size), :]
        copies.append(pltpu.make_async_copy(rows_ref.at[rows, :], target, sems.at[i]))
        copies[-1].start()
    for copy in copies:
        copy.wait()


def row_move(value, bit):
    count = lax.axis_size("row")
    return lax.ppermute(value, "row", [(s, s ^ bit) for s in range(count)])


def col_shift(value, steps):
    count = lax.axis_size("col")
    return lax.ppermute(value, "col", [(s, (s + steps) % count) for s in range(count)])


def column_pieces(width, count):
    lanes = width // 128
    sizes = [lanes // count + (p < lanes % count) for p in range(count)]
    return [128 * size for size in sizes]


def sds(rows, width, dtype):
    return jax.ShapeDtypeStruct((rows, width), dtype)


def shards(messages, targets, reverse_rows, nodes, w_in, w_res, w_node):
    m = messages[0, 0]
    order = reverse_rows[0, 0]
    share_h = nodes[0]
    edges, width = m.shape
    share = share_h.shape[0]
    blocks, block = order.shape
    pair_rows = 2 * block
    count = lax.axis_size("row")
    assert count & (count - 1) == 0
    points = count * share
    scale = 1.0 / math.sqrt(edges // share)
    me = lax.axis_index("row").astype(jnp.int32)
    layers = w_in.shape[0]
    product = 2 * pair_rows * width * width
    rounds = count.bit_length() - 1
    pieces = column_pieces(width, rounds)
    piece_shapes = [sds(points, piece, t) for piece in pieces for t in (F32, BF16)]
    own = partner_numbers(targets[0], me, share)
    table = [share_h]
    m, *sums = call(
        partial_body,
        [sds(edges, width, BF16)] + piece_shapes,
        (own, m),
        2 * points * edges * width,
    )
    w_in, w_res, w_node, order, *sums = lax.optimization_barrier(
        (w_in, w_res, w_node, order, *sums)
    )
    for k in range(1, count):
        table.append(row_move(share_h, k))
    hot = (own[0][:, None] == jnp.arange(points, dtype=jnp.int32)[None, :]).astype(BF16)
    groups = (tuple(range(2, blocks - 2)), tuple(range(blocks - 2, blocks)))
    m_parts = [(m, 0)] + [(m, ks[0] * block) for ks in groups]
    for layer in range(layers):
        first, last = layer == 0, layer == layers - 1
        for r in range(rounds):
            bits = [1 << ((p + r) % rounds) for p in range(rounds)]
            got = []
            for p, bit in enumerate(bits):
                got.append(row_move(sums[2 * p + 1], bit))
            if r < rounds - 1:
                sums = call(
                    functools.partial(add_body, bits, share),
                    piece_shapes,
                    (*sums[::2], *got),
                    points * width,
                )
        if first:
            (hot_sent,) = call(
                order_body,
                [sds(edges, points, BF16)],
                (order, hot),
                2 * edges * block * points,
            )
        (pre,) = call(
            functools.partial(pre_body, layer),
            [sds(edges, width, F32)],
            (order, *((m,) if first else [part for part, _ in m_parts]), w_in),
            PAIRS * product,
        )
        h, *outs = call(
            functools.partial(update_body, bits, share, scale, layer, 4),
            [sds(points, width, BF16)] + [sds(block, width, BF16)] * 2,
            (w_node[layer], hot_sent, pre, w_in, *sums[::2], *got, *table),
            2 * points * width * width + 2 * product,
        )
        table = [h]
        sent = {}
        for pair in (2, 1, 3):
            if pair != 2:
                outs = call(
                    functools.partial(send_body, layer, 2 * pair),
                    [sds(block, width, BF16)] * 2,
                    (hot_sent, pre, w_in, h),
                    2 * product,
                )
            for half, out in enumerate(outs):
                k = 2 * pair + half
                sent[k ^ 1] = col_shift(out, OFFSETS[k])
        out = call(
            functools.partial(local_body, layer, last),
            [sds(edges - pair_rows, width, F32), sds(pair_rows, width, BF16)]
            + [sds(share, width, BF16) if last else sds(points, width, F32)],
            (hot, hot_sent, pre, h, m_parts[0][0], w_in, w_res) + (() if last else (own,)),
            12 * product,
        )
        part, done, sums = out[0], [out[1]], [out[2]]
        if last:
            share_h = out[2]
        for name, ks, (source, at) in zip(("near", "far"), groups, m_parts[1:]):
            where = (layer, at, ks[0] * block, ks[0] * block - pair_rows, len(ks))
            got = [sent[k] for k in ks]
            if last:
                done = call(
                    functools.partial(last_body, *where),
                    [sds(edges, width, BF16)],
                    (part, source, w_res, *got, *done),
                    2 * len(ks) * product,
                    spaces={3 + len(ks): pltpu.HBM} if name == "far" else {},
                    out_space=pltpu.HBM,
                    scratch=(
                        pltpu.VMEM((len(ks) * block, width), BF16),
                        pltpu.SemaphoreType.DMA((len(ks) + 1,)),
                    ),
                    aliases={3 + len(ks): 0} if name == "far" else {},
                )
            else:
                new, *sums = call(
                    functools.partial(edge_body, *where),
                    [sds(len(ks) * block, width, BF16)]
                    + (piece_shapes if name == "far" else [sds(points, width, F32)]),
                    (part, source, w_res, own, *sums, *got),
                    3 * len(ks) * product,
                )
                done.append(new)
        m_parts = [(new, 0) for new in done]
    return (done[0][None, None], share_h[None])


def solution(mesh):
    in_specs = (
        P("row", "col", None, None),
        P("row", "col", None),
        P("row", "col", None, None),
        P("col", "row", None),
        P(),
        P(),
        P(),
    )
    out_specs = (P("row", "col", None, None), P("col", "row", None))
    return jax.shard_map(shards, mesh=mesh, in_specs=in_specs, out_specs=out_specs, check_vma=False)
```
